256 devices in a mesh: seq: 128 (over z, x_lo, y, core), dp: 2 (over x_hi).
Axes of the slice: x: 4 (x_hi: 2, x_lo: 2; x = x_hi * 2 + x_lo), y: 4, z: 8, core: 2. Of those that a mesh axis runs over, the one named last changes fastest.
Arguments:
- genome: bfloat16 [2, 262144, 512], P('dp', 'seq'), may hold values from -6 to 6
- conv_weight: bfloat16 [3, 512, 512], replicated, may hold values from -0.15625 to 0.15625
- upstream: bfloat16 [2, 262144, 512], P('dp', 'seq'), may hold values from -6 to 6
Outputs:
- output: bfloat16 [2, 262144, 512], P('dp', 'seq')
- grad_genome: bfloat16 [2, 262144, 512], P('dp', 'seq')
- grad_weight: float32 [3, 512, 512], replicated
The draws below stay inside these ranges and needn't reach their ends.
All inputs are finite; a program needn't handle non-finite values.
Results may differ from the reference program's by a relative error of at most 0.0035.
Values may be sent and summed in bfloat16 or wider, within the bound.
A program may use at most 128 MiB of HBM per device.

```python
import jax
import jax.numpy as jnp
from jax import lax

C = 512
DILATION_BINS = 4096
BINS = 262144
GENOMES = 2


def block_scale(own_key, dims, split, least, high):
    loudness = 1.0
    for position, parts in split:
        draws = jax.random.uniform(jax.random.fold_in(jax.random.fold_in(own_key, 6), position), (parts,), jnp.float32, least / len(split), high / len(split))
        loudness = loudness * jnp.repeat(jnp.exp(draws), dims[position] // parts).reshape((-1,) + (1,) * (len(dims) - 1 - position))
    return loudness


def scatter_about(rng, extent, width, reach, shards=(), kind=jnp.bfloat16):
    loudness = block_scale(rng, extent, shards, -0.22, 0.18) if shards else 1.0
    array = jax.random.normal(rng, extent, jnp.float32) * width * loudness
    return jnp.minimum(jnp.maximum(array, -reach), reach).astype(kind)


def setup_inputs(seed: int = 0) -> dict:
    keys = jax.random.split(jax.random.key(seed), 4)
    genome = scatter_about(keys[0], (GENOMES, BINS, C), 1.0, 6.0, ((0, 2), (1, 128)))
    conv_weight = scatter_about(keys[1], (3, C, C), (3 * C) ** -0.5, 0.15625)
    upstream = scatter_about(keys[2], (GENOMES, BINS, C), 1.0, 6.0, ((0, 2), (1, 128)))
    return dict(genome=genome, conv_weight=conv_weight, upstream=upstream)


def taps(receptive_field):
    padded_input = jnp.pad(receptive_field, ((0, 0), (DILATION_BINS, DILATION_BINS), (0, 0)))
    return (padded_input[:, :-2 * DILATION_BINS], padded_input[:, 2 * DILATION_BINS:])

def mixing(left, right):
    return jnp.einsum('gbc,cd->gbd', left, right, precision=lax.Precision.HIGHEST)

def outer_sum(left, right):
    return jnp.einsum('gbc,gbd->cd', left, right, precision=lax.Precision.HIGHEST)

def reference(genome, conv_weight, upstream):
    inputs = genome.astype(jnp.float32)
    act_full, slope_fn = jax.vjp(jax.nn.gelu, inputs)
    act = act_full.astype(jnp.bfloat16).astype(jnp.float32)
    act_prev, act_next = taps(act)
    weights = conv_weight.astype(jnp.float32)
    conv = mixing(act_prev, weights[0]) + mixing(act, weights[1]) + mixing(act_next, weights[2])
    output = (inputs + conv).astype(jnp.bfloat16)
    grads = upstream.astype(jnp.float32)
    up_prev, up_next = taps(grads)
    grad_act = mixing(up_next, weights[0].T) + mixing(grads, weights[1].T) + mixing(up_prev, weights[2].T)
    grad_genome = (grads + slope_fn(grad_act)[0]).astype(jnp.bfloat16)
    grad_weight = jnp.stack([outer_sum(act_prev, grads), outer_sum(act, grads), outer_sum(act_next, grads)])
    return (output, grad_genome, grad_weight)
```

```python
import functools

import jax
import jax.numpy as jnp
from jax import lax
from jax.experimental import pallas as pl
from jax.experimental.pallas import tpu as pltpu
from jax.sharding import PartitionSpec as P

MESH = pl.DeviceIdType.MESH
F32 = jnp.float32
BF16 = jnp.bfloat16
DILATION_BINS = 4096
NCH = 8
NGC = 16
AHEAD = 2
CUBIC = 0.044715
SLOPE = 0.7978845608028654


def gelu(x):
    return x * (0.5 * (1.0 + jnp.tanh(SLOPE * (x + CUBIC * (x * x * x)))))


def gelu_slope(x):
    square = x * x
    t = jnp.tanh(SLOPE * (x + CUBIC * (x * square)))
    return 0.5 * (1.0 + t) + (0.5 * SLOPE) * x * (1.0 - t * t) * (1.0 + (3.0 * CUBIC) * square)


def dot(a, b):
    return jnp.dot(a, b, preferred_element_type=F32)


def dot_nt(a, b):
    return lax.dot_general(a, b, (((1,), (1,)), ((), ())), preferred_element_type=F32)


def kernel(
    dims, hop,
    g_hbm, w_hbm, u_hbm, out_hbm, gg_hbm, gw_hbm,
    g, u, w, u_prev, u_next, g_prev, g_next, act, act_t, ob, gb,
    acc, rc, xs, rx, zs, rz, ry, ag, gwf,
    lsem, us, ur, gs, gr, osem, gsem, wsem,
    cs, cr, xss, xr, zss, zr, yss, yr, azs, azr, axs, axr, acs, acr,
):
    nz, nxl, ny, nd = dims
    nx = nxl * nd
    ns = nz * nxl * ny * 2
    bins, chans = g.shape
    rows = 3 * chans
    rx_rows = rows // nx
    rz_rows = rx_rows // nz
    ch, gch = bins // NCH, bins // NGC
    wide = chans // 2
    half = wide // 2

    s = lax.axis_index("seq")
    d = lax.axis_index("dp")
    core = lax.rem(s, 2)
    y = lax.rem(lax.div(s, 2), ny)
    xl = lax.rem(lax.div(s, 2 * ny), nxl)
    z = lax.div(s, 2 * ny * nxl)
    x = d * nxl + xl

    def at(z_, x_, y_, c_):
        return {
            "dp": lax.div(x_, nxl),
            "seq": ((z_ * nxl + lax.rem(x_, nxl)) * ny + y_) * 2 + c_,
        }

    after = {"dp": d, "seq": lax.rem(s + hop, ns)}
    before = {"dp": d, "seq": lax.rem(s + ns - hop, ns)}
    partner = at(z, x, y, 1 - core)

    def x_at(k):
        return lax.rem(x + 1 + k, nx)

    def x_from(k):
        return lax.rem(x + 2 * nx - 1 - k, nx)

    def z_at(k):
        return lax.rem(z + 1 + k, nz)

    def z_from(k):
        return lax.rem(z + 2 * nz - 1 - k, nz)

    def y_at(k):
        return lax.rem(y + 1 + k, ny)

    def y_from(k):
        return lax.rem(y + 2 * ny - 1 - k, ny)

    x_peers = [at(z, x_at(k), y, core) for k in range(nx - 1)]
    z_peers = [at(z_at(k), x, y, core) for k in range(nz - 1)]
    y_peers = [at(z, x, y_at(k), core) for k in range(ny - 1)]

    def ds(start, size, step):
        return pl.ds(pl.multiple_of(start, step), size)

    def remote(src, dst, send, recv, device):
        return pltpu.make_async_remote_copy(
            src_ref=src, dst_ref=dst, send_sem=send, recv_sem=recv, device_id=device, device_id_type=MESH
        )

    loads = [
        pltpu.make_async_copy(g_hbm, g, lsem.at[0]),
        pltpu.make_async_copy(u_hbm, u, lsem.at[1]),
        pltpu.make_async_copy(w_hbm, w, lsem.at[2]),
    ]
    for load in loads:
        load.start()

    barrier = pltpu.get_barrier_semaphore()
    greeted = [after, before, partner] + x_peers + z_peers + y_peers
    for device in greeted:
        pl.semaphore_signal(barrier, inc=1, device_id=device, device_id_type=MESH)
    pl.semaphore_wait(barrier, len(greeted))

    def up_copy(j, i, way):
        block = (ds(i * ch, ch, ch), pl.ds(j * wide, wide))
        dst = (u_prev, u_next)[way]
        return remote(
            u_hbm.at[block], dst.at[block], us.at[way, j, i], ur.at[way, j, i], (after, before)[way]
        )

    def genome_copy(i, way):
        block = ds(i * gch, gch, gch)
        dst = (g_prev, g_next)[way]
        return remote(g_hbm.at[block], dst.at[block], gs.at[way, i], gr.at[way, i], (after, before)[way])

    def send_genome(i):
        for way in range(2):
            genome_copy(i, way).start()

    for j in range(2):

        def send_up(i, _, j=j):
            for way in range(2):
                up_copy(j, i, way).start()
            return 0

        lax.fori_loop(0, NCH, send_up, 0)

    def c_copy(j, k):
        block = ds(x_at(k) * rx_rows, rx_rows, rx_rows)
        return remote(
            acc.at[j, 1 - core, block], rc.at[j, block], cs.at[j, k], cr.at[j, k], partner
        )

    def x_copy(j, k):
        block = ds(x_at(k) * rx_rows, rx_rows, rx_rows)
        return remote(xs.at[j, block], rx.at[j, k], xss.at[j, k], xr.at[j, k], x_peers[k])

    def z_copy(j, k):
        block = ds(z_at(k) * rz_rows, rz_rows, rz_rows)
        return remote(zs.at[j, block], rz.at[j, k], zss.at[j, k], zr.at[j, k], z_peers[k])

    def y_copy(j, k, slot):
        return remote(ry.at[j, slot], ry.at[j, slot], yss.at[j, k], yr.at[j, k], y_peers[k])

    def az_copy(j, k, z_):
        block = ag.at[j, core, ds(x * rx_rows + z_ * rz_rows, rz_rows, rz_rows)]
        return remote(block, block, azs.at[j, k], azr.at[j, k], z_peers[k])

    def ax_copy(j, k, x_):
        block = ag.at[j, core, ds(x_ * rx_rows, rx_rows, rx_rows)]
        return remote(block, block, axs.at[j, k], axr.at[j, k], x_peers[k])

    def ac_copy(j, c_):
        return remote(ag.at[j, c_], ag.at[j, c_], acs.at[j], acr.at[j], partner)

    def send_c(j):
        for k in range(nx):
            c_copy(j, k).start()

    def send_x(j):
        for k in range(nx - 1):
            c_copy(j, k).wait_recv()
            block = ds(x_at(k) * rx_rows, rx_rows, rx_rows)
            xs[j, block] = (acc[j, core, block] + rc[j, block]).astype(BF16)
            x_copy(j, k).start()

    def send_z(j):
        c_copy(j, nx - 1).wait_recv()
        block = ds(x * rx_rows, rx_rows, rx_rows)
        for k in range(nx - 1):
            x_copy(j, k).wait_recv()
        total = acc[j, core, block] + rc[j, block]
        for k in range(nx - 1):
            total += rx[j, k].astype(F32)
        zs[j] = total
        for k in range(nz - 1):
            z_copy(j, k).start()

    def send_y(j):
        for k in range(nz - 1):
            z_copy(j, k).wait_recv()
        total = zs[j, ds(z * rz_rows, rz_rows, rz_rows)]
        for k in range(nz - 1):
            total += rz[j, k]
        ry[j, y] = total
        for k in range(ny - 1):
            y_copy(j, k, y).start()

    def send_az(j):
        for k in range(ny - 1):
            y_copy(j, k, y_from(k)).wait_recv()
        total = ry[j, 0]
        for k in range(1, ny):
            total += ry[j, k]
        ag[j, core, ds(x * rx_rows + z * rz_rows, rz_rows, rz_rows)] = total.astype(BF16)
        for k in range(nz - 1):
            az_copy(j, k, z).start()

    def send_ax(j):
        for k in range(nz - 1):
            az_copy(j, k, z_from(k)).wait_recv()
        for k in range(nx - 1):
            ax_copy(j, k, x).start()

    def send_ac(j):
        for k in range(nx - 1):
            ax_copy(j, k, x_from(k)).wait_recv()
        ac_copy(j, core).start()

    def gw_copy(j):
        columns = pl.ds(j * wide, wide)
        return pltpu.make_async_copy(gwf.at[:, :, columns], gw_hbm.at[:, :, columns], wsem.at[j])

    def finish(j):
        ac_copy(j, 1 - core).wait_recv()
        for h in range(2):
            for k in range(3):
                gwf[k, :, pl.ds(j * wide + h * half, half)] = ag[j, h, pl.ds(k * chans, chans)].astype(F32)
        gw_copy(j).start()

    has_prev = jnp.where(s >= hop, 1.0, 0.0).astype(F32)
    has_next = jnp.where(s < ns - hop, 1.0, 0.0).astype(F32)

    for load in loads:
        load.wait()
    acc[...] = jnp.zeros_like(acc)

    def own(i, _):
        block = ds(i * gch, gch, gch)
        a = gelu(g[block].astype(F32))
        act[block] = a.astype(BF16)
        act_t[:, block] = a.T.astype(BF16)
        return 0

    lax.fori_loop(0, NGC, own, 0)

    def masked(ref, index, there):
        value = ref[index]
        return value * jnp.full(value.shape, there, F32).astype(BF16)

    def gg_copy(i):
        block = ds(i * ch, ch, ch)
        return pltpu.make_async_copy(gb.at[block], gg_hbm.at[block], gsem.at[i])

    def out_copy(i):
        block = ds(i * gch, gch, gch)
        return pltpu.make_async_copy(ob.at[block], out_hbm.at[block], osem.at[i])

    def staged(i, stages):
        for tick, stage, j in stages:
            pl.when(i == tick)(functools.partial(stage, j))

    def up_step(j, stages):
        def body(i, _):
            for way in range(2):
                up_copy(j, i, way).wait_recv()
            block = ds(i * ch, ch, ch)
            columns = pl.ds(j * wide, wide)
            left = act_t[:, block]
            for tap, right in (
                (0, masked(u_next, (block, columns), has_next)),
                (1, u[block, columns]),
                (2, masked(u_prev, (block, columns), has_prev)),
            ):
                term = dot(left, right)
                span = pl.ds(tap * chans, chans)
                acc[j, 0, span] += term[:, :half]
                acc[j, 1, span] += term[:, half:]
            if j == 1:
                own_up = u[block]
                grad_act = (
                    dot_nt(masked(u_next, block, has_next), w[0])
                    + dot_nt(own_up, w[1])
                    + dot_nt(masked(u_prev, block, has_prev), w[2])
                )
                slope = gelu_slope(g[block].astype(F32))
                gb[block] = (own_up.astype(F32) + slope * grad_act).astype(BF16)
                gg_copy(i).start()
            staged(i, stages)
            return 0

        lax.fori_loop(0, NCH, body, 0)

    def send_first(_):
        for i in range(AHEAD):
            send_genome(i)

    up_step(0, ())
    send_c(0)
    up_step(1, ((0, send_x, 0), (4, send_first, 0), (5, send_z, 0)))
    send_c(1)

    stages = (
        (0, send_x, 1),
        (2, send_y, 0),
        (4, send_z, 1),
        (5, send_az, 0),
        (7, send_y, 1),
        (8, send_ax, 0),
        (10, send_az, 1),
        (11, send_ac, 0),
        (12, finish, 0),
        (13, send_ax, 1),
        (15, send_ac, 1),
    )

    def genome_step(i, _):
        for way in range(2):
            genome_copy(i, way).wait_recv()
        pl.when(i + AHEAD < NGC)(lambda: send_genome(i + AHEAD))
        block = ds(i * gch, gch, gch)
        a_prev = gelu(g_prev[block].astype(F32) * has_prev).astype(BF16)
        a_next = gelu(g_next[block].astype(F32) * has_next).astype(BF16)
        conv = dot(a_prev, w[0]) + dot(act[block], w[1]) + dot(a_next, w[2])
        ob[block] = (g[block].astype(F32) + conv).astype(BF16)
        out_copy(i).start()
        staged(i, stages)
        return 0

    lax.fori_loop(0, NGC, genome_step, 0)
    finish(1)

    def drain_up(i, _):
        for way in range(2):
            for j in range(2):
                up_copy(j, i, way).wait_send()
        gg_copy(i).wait()
        return 0

    lax.fori_loop(0, NCH, drain_up, 0)

    def drain_genome(i, _):
        for way in range(2):
            genome_copy(i, way).wait_send()
        out_copy(i).wait()
        return 0

    lax.fori_loop(0, NGC, drain_genome, 0)
    for j in range(2):
        for k in range(nx):
            c_copy(j, k).wait_send()
        for k in range(nx - 1):
            x_copy(j, k).wait_send()
            ax_copy(j, k, x).wait_send()
        for k in range(nz - 1):
            z_copy(j, k).wait_send()
            az_copy(j, k, z).wait_send()
        for k in range(ny - 1):
            y_copy(j, k, y).wait_send()
        ac_copy(j, core).wait_send()
        gw_copy(j).wait()


def per_device(dims, genome, conv_weight, upstream):
    nz, nxl, ny, nd = dims
    nx = nxl * nd
    _, bins, chans = genome.shape
    rows, half = 3 * chans, chans // 4
    hop = DILATION_BINS // bins
    dma = pltpu.SemaphoreType.DMA
    block = pltpu.VMEM((bins, chans), BF16)
    out, grad_genome, grad_weight = pl.pallas_call(
        functools.partial(kernel, dims, hop),
        out_shape=(
            jax.ShapeDtypeStruct((bins, chans), BF16),
            jax.ShapeDtypeStruct((bins, chans), BF16),
            jax.ShapeDtypeStruct((3, chans, chans), F32),
        ),
        in_specs=[pl.BlockSpec(memory_space=pl.ANY)] * 3,
        out_specs=(pl.BlockSpec(memory_space=pl.ANY),) * 3,
        scratch_shapes=[
            block, block,
            pltpu.VMEM((3, chans, chans), BF16),
            block, block, block, block, block,
            pltpu.VMEM((chans, bins), BF16),
            block, block,
            pltpu.VMEM((2, 2, rows, half), F32),
            pltpu.VMEM((2, rows, half), F32),
            pltpu.VMEM((2, rows, half), BF16),
            pltpu.VMEM((2, nx - 1, rows // nx, half), BF16),
            pltpu.VMEM((2, rows // nx, half), F32),
            pltpu.VMEM((2, nz - 1, rows // nx // nz, half), F32),
            pltpu.VMEM((2, ny, rows // nx // nz, half), F32),
            pltpu.VMEM((2, 2, rows, half), BF16),
            pltpu.VMEM((3, chans, chans), F32),
            dma((3,)),
            dma((2, 2, NCH)), dma((2, 2, NCH)),
            dma((2, NGC)), dma((2, NGC)),
            dma((NGC,)), dma((NCH,)), dma((2,)),
            dma((2, nx)), dma((2, nx)),
            dma((2, nx - 1)), dma((2, nx - 1)),
            dma((2, nz - 1)), dma((2, nz - 1)),
            dma((2, ny - 1)), dma((2, ny - 1)),
            dma((2, nz - 1)), dma((2, nz - 1)),
            dma((2, nx - 1)), dma((2, nx - 1)),
            dma((2,)), dma((2,)),
        ],
        compiler_params=pltpu.CompilerParams(
            collective_id=0, has_side_effects=True, vmem_limit_bytes=60 * 1024 * 1024
        ),
    )(genome.reshape(bins, chans), conv_weight, upstream.reshape(bins, chans))
    return out.reshape(genome.shape), grad_genome.reshape(genome.shape), grad_weight


def solution(mesh):
    ny, nxl, nc = 4, 2, 2
    nz = mesh.shape["seq"] // (ny * nxl * nc)
    return jax.shard_map(
        functools.partial(per_device, (nz, nxl, ny, mesh.shape["dp"])),
        mesh=mesh,
        in_specs=(P("dp", "seq", None), P(), P("dp", "seq", None)),
        out_specs=(P("dp", "seq", None), P("dp", "seq", None), P()),
        check_vma=False,
    )
```

```python
import functools

import jax
import jax.numpy as jnp
from jax import lax
from jax.experimental import pallas as pl
from jax.experimental.pallas import tpu as pltpu
from jax.sharding import PartitionSpec as P

MESH = pl.DeviceIdType.MESH
F32 = jnp.float32
BF16 = jnp.bfloat16
DILATION_BINS = 4096
NCH = 4
NGC = 16
GROUPS = 4
EARLY = 4
LATE = 9
VMEM_MIB = 46
CUBIC = 0.044715
SLOPE = 0.7978845608028654


def gelu(x):
    return x * (0.5 * (1.0 + jnp.tanh(SLOPE * (x + CUBIC * (x * x * x)))))


def gelu_slope(x):
    square = x * x
    t = jnp.tanh(SLOPE * (x + CUBIC * (x * square)))
    return 0.5 * (1.0 + t) + (0.5 * SLOPE) * x * (1.0 - t * t) * (1.0 + (3.0 * CUBIC) * square)


def dot(a, b):
    return jnp.dot(a, b, preferred_element_type=F32)


def dot_nt(a, b):
    return lax.dot_general(a, b, (((1,), (1,)), ((), ())), preferred_element_type=F32)


def kernel(
    dims, hop,
    g_hbm, w_hbm, u_hbm, out_hbm, gg_hbm, gw_hbm,
    g, u, w, u_other, g_other, u_prev, u_next, g_prev, g_next, act, act_t, ob, gb,
    acc, rc, os_, orx, is_, irx, zf, zs, rz, ry, ag,
    lsem, ous, our, ogs, ogr, us, ur, gs, gr, osem, gsem, wsem,
    cs, cr, oss, osr, iss, isr, zss, zr, yss, yr, azs, azr, ais, air, aos, aor, acs, acr, ysem,
):
    nz, nxl, ny, nd = dims
    nx = nxl * nd
    ns = nz * nxl * ny * 2
    bins, chans = g.shape
    rows = 3 * chans
    rx_rows = rows // nx
    rz_rows = rx_rows // nz
    ch, gch = bins // NCH, bins // NGC
    wide = chans // GROUPS

    s = lax.axis_index("seq")
    d = lax.axis_index("dp")
    core = lax.rem(s, 2)
    y = lax.rem(lax.div(s, 2), ny)
    xl = lax.rem(lax.div(s, 2 * ny), nxl)
    z = lax.div(s, 2 * ny * nxl)
    x = d * nxl + xl
    base = s - core
    moves, sums = core == 0, core == 1

    def at(z_, x_, y_, c_):
        return {
            "dp": lax.div(x_, nxl),
            "seq": ((z_ * nxl + lax.rem(x_, nxl)) * ny + y_) * 2 + c_,
        }

    def beside(way, c_):
        return {"dp": d, "seq": lax.rem(base + (hop, ns - hop)[way], ns) + c_}

    partner = at(z, x, y, 1 - core)

    outer_x = lax.rem(x + 3 - 2 * xl, nx)
    inner_x = x + 1 - 2 * xl
    outer, inner = at(z, outer_x, y, core), at(z, inner_x, y, core)

    def z_at(k):
        return lax.rem(z + 1 + k, nz)

    def z_from(k):
        return lax.rem(z + 2 * nz - 1 - k, nz)

    def y_at(k):
        return lax.rem(y + 1 + k, ny)

    def y_from(k):
        return lax.rem(y + 2 * ny - 1 - k, ny)

    z_peers = [at(z_at(k), x, y, core) for k in range(nz - 1)]
    y_peers = [at(z, x, y_at(k), core) for k in range(ny - 1)]

    def ds(start, size, step):
        return pl.ds(pl.multiple_of(start, step), size)

    def remote(src, dst, send, recv, device):
        return pltpu.make_async_remote_copy(
            src_ref=src, dst_ref=dst, send_sem=send, recv_sem=recv, device_id=device, device_id_type=MESH
        )

    loads = [
        pltpu.make_async_copy(g_hbm, g, lsem.at[0]),
        pltpu.make_async_copy(u_hbm, u, lsem.at[1]),
        pltpu.make_async_copy(w_hbm, w, lsem.at[2]),
    ]
    for load in loads:
        load.start()

    barrier = pltpu.get_barrier_semaphore()

    def greet(devices):
        for device in devices:
            pl.semaphore_signal(barrier, inc=1, device_id=device, device_id_type=MESH)

    greet([partner, beside(0, 0), beside(1, 0)])
    sum_peers = z_peers + y_peers + [outer, inner]

    @pl.when(moves)
    def _():
        pl.semaphore_wait(barrier, 5)

    @pl.when(sums)
    def _():
        greet(sum_peers)
        pl.semaphore_wait(barrier, 1 + len(sum_peers))

    def columns(j):
        return pl.ds(j * wide, wide)

    def up_block(j, i):
        return (ds(i * ch, ch, ch), columns(j))

    def up_copy(j, i, way, c_):
        block = up_block(j, i)
        src, dst = (u_hbm, u_other)[c_], (u_prev, u_next)[way]
        return remote(
            src.at[block], dst.at[block], us.at[c_, way, j, i], ur.at[way, j, i], beside(way, c_)
        )

    def up_handed(j, i):
        block = up_block(j, i)
        return remote(u_hbm.at[block], u_other.at[block], ous.at[j, i], our.at[j, i], partner)

    def genome_copy(i, way, c_):
        block = ds(i * gch, gch, gch)
        src, dst = (g_hbm, g_other)[c_], (g_prev, g_next)[way]
        return remote(src.at[block], dst.at[block], gs.at[c_, way, i], gr.at[way, i], beside(way, c_))

    def genome_handed(i):
        block = ds(i * gch, gch, gch)
        return remote(g_hbm.at[block], g_other.at[block], ogs.at[i], ogr.at[i], partner)

    @pl.when(sums)
    def _():
        for j in range(GROUPS):

            def hand_up(i, _, j=j):
                up_handed(j, i).start()
                return 0

            lax.fori_loop(0, NCH, hand_up, 0)

        def hand_genome(i, _):
            genome_handed(i).start()
            return 0

        lax.fori_loop(0, NGC, hand_genome, 0)

    @pl.when(moves)
    def _():
        for j in range(GROUPS):

            def send_up(i, _, j=j):
                for way in range(2):
                    up_copy(j, i, way, 0).start()
                up_handed(j, i).wait_recv()
                for way in range(2):
                    up_copy(j, i, way, 1).start()
                return 0

            lax.fori_loop(0, NCH, send_up, 0)

    def x_block(x_):
        return ds(x_ * rx_rows, rx_rows, rx_rows)

    def z_block(z_):
        return ds(z_ * rz_rows, rz_rows, rz_rows)

    def c_block(k):
        return x_block((2 * (1 - d), 2 * (1 - d) + 1, inner_x, x)[k])

    def c_copy(j, k):
        block = c_block(k)
        return remote(acc.at[j, block], rc.at[j, block], cs.at[j, k], cr.at[j, k], partner)

    def o_copy(j, k):
        return remote(os_.at[j, k], orx.at[j, k], oss.at[j, k], osr.at[j, k], outer)

    def i_copy(j):
        return remote(is_.at[j], irx.at[j], iss.at[j], isr.at[j], inner)

    def z_copy(j, k):
        return remote(zs.at[j, z_block(z_at(k))], rz.at[j, k], zss.at[j, k], zr.at[j, k], z_peers[k])

    def y_copy(j, k, slot):
        return remote(ry.at[j, slot], ry.at[j, slot], yss.at[j, k], yr.at[j, k], y_peers[k])

    def az_copy(j, k, z_):
        block = ag.at[ds(x * rx_rows + z_ * rz_rows, rz_rows, rz_rows), columns(j)]
        return remote(block, block, azs.at[j, k], azr.at[j, k], z_peers[k])

    def ai_copy(j, x_):
        block = ag.at[x_block(x_), columns(j)]
        return remote(block, block, ais.at[j], air.at[j], inner)

    def ao_copy(j, k, d_):
        block = ag.at[x_block(2 * d_ + k), columns(j)]
        return remote(block, block, aos.at[j, k], aor.at[j, k], outer)

    def ac_copy(j, k, x_):
        block = ag.at[x_block(x_), columns(j)]
        return remote(block, block, acs.at[j, k], acr.at[j, k], partner)

    def send_c(j):
        @pl.when(moves)
        def _():
            for k in range(nx):
                c_copy(j, k).start()

    def send_o(j):
        for k in range(2):
            c_copy(j, k).wait_recv()
            block = c_block(k)
            os_[j, k] = acc[j, block] + rc[j, block]
            o_copy(j, k).start()

    def send_i(j):
        c_copy(j, 2).wait_recv()
        o_copy(j, 1 - xl).wait_recv()
        block = c_block(2)
        is_[j] = (acc[j, block] + rc[j, block] + orx[j, 1 - xl]).astype(BF16)
        i_copy(j).start()

    def send_z(j):
        c_copy(j, 3).wait_recv()
        o_copy(j, xl).wait_recv()
        i_copy(j).wait_recv()
        block = c_block(3)
        total = acc[j, block] + rc[j, block] + orx[j, xl] + irx[j].astype(F32)
        zf[j] = total
        zs[j] = total.astype(BF16)
        for k in range(nz - 1):
            z_copy(j, k).start()

    def send_y(j):
        for k in range(nz - 1):
            z_copy(j, k).wait_recv()
        total = zf[j, z_block(z)]
        for k in range(nz - 1):
            total += rz[j, k].astype(F32)
        ry[j, y] = total
        for k in range(ny - 1):
            y_copy(j, k, y).start()
        pl.semaphore_signal(ysem.at[j], inc=1, device_id=partner, device_id_type=MESH)

    def send_az(j):
        for k in range(ny - 1):
            y_copy(j, k, y_from(k)).wait_recv()
        total = ry[j, 0]
        for k in range(1, ny):
            total += ry[j, k]
        ag[ds(x * rx_rows + z * rz_rows, rz_rows, rz_rows), columns(j)] = total.astype(BF16)
        for k in range(nz - 1):
            az_copy(j, k, z).start()

    def send_ai(j):
        for k in range(nz - 1):
            az_copy(j, k, z_from(k)).wait_recv()
        ai_copy(j, x).start()
        ao_copy(j, xl, d).start()
        ac_copy(j, 3, x).start()

    def send_ao(j):
        ai_copy(j, inner_x).wait_recv()
        ao_copy(j, 1 - xl, d).start()
        ac_copy(j, 2, inner_x).start()

    def send_ac(j):
        for k in range(2):
            ao_copy(j, k, 1 - d).wait_recv()
            ac_copy(j, k, 2 * (1 - d) + k).start()

    def gw_copy(j):
        return pltpu.make_async_copy(ag.at[:, columns(j)], gw_hbm.at[:, columns(j)], wsem.at[j])

    def finish(j):
        @pl.when(moves)
        def _():
            for k, x_ in enumerate((2 * (1 - d), 2 * (1 - d) + 1, inner_x, x)):
                ac_copy(j, k, x_).wait_recv()

        gw_copy(j).start()

    has_prev = jnp.where(s >= hop, 1.0, 0.0).astype(F32)
    has_next = jnp.where(s < ns - hop, 1.0, 0.0).astype(F32)

    for load in loads:
        load.wait()
    acc[...] = jnp.zeros_like(acc)

    def own(i, _):
        block = ds(i * gch, gch, gch)
        a = gelu(g[block].astype(F32))
        act[block] = a.astype(BF16)
        act_t[:, block] = a.T.astype(BF16)
        return 0

    lax.fori_loop(0, NGC, own, 0)

    def send_genome(i, _):
        for way in range(2):
            genome_copy(i, way, 0).start()
        genome_handed(i).wait_recv()
        for way in range(2):
            genome_copy(i, way, 1).start()
        return 0

    @pl.when(moves)
    def _():
        lax.fori_loop(0, EARLY, send_genome, 0)

    def go_on(first, last, groups):
        for j in groups:
            pl.semaphore_wait(ysem.at[j], 1)
        lax.fori_loop(first, last, send_genome, 0)

    def masked(ref, index, there):
        value = ref[index]
        return value * jnp.full(value.shape, there, F32).astype(BF16)

    def gg_copy(i):
        block = ds(i * ch, ch, ch)
        return pltpu.make_async_copy(gb.at[block], gg_hbm.at[block], gsem.at[i])

    def out_copy(i):
        block = ds(i * gch, gch, gch)
        return pltpu.make_async_copy(ob.at[block], out_hbm.at[block], osem.at[i])

    def staged(i, stages):
        for tick, stage, groups in stages:
            when = i == tick
            if stage is not finish:
                when = jnp.logical_and(when, sums)

            @pl.when(when)
            def _(stage=stage, groups=groups):
                for j in groups if isinstance(groups, tuple) else (groups,):
                    stage(j)

    def up_step(j, stages):
        def body(i, _):
            for way in range(2):
                up_copy(j, i, way, 0).wait_recv()
            block, side = up_block(j, i)
            left = act_t[:, block]
            for tap, right in (
                (0, masked(u_next, (block, side), has_next)),
                (1, u[block, side]),
                (2, masked(u_prev, (block, side), has_prev)),
            ):
                acc[j, pl.ds(tap * chans, chans)] += dot(left, right)
            if j == GROUPS - 1:
                own_up = u[block]
                grad_act = (
                    dot_nt(masked(u_next, block, has_next), w[0])
                    + dot_nt(own_up, w[1])
                    + dot_nt(masked(u_prev, block, has_prev), w[2])
                )
                slope = gelu_slope(g[block].astype(F32))
                gb[block] = (own_up.astype(F32) + slope * grad_act).astype(BF16)
                gg_copy(i).start()
            staged(i, stages)
            return 0

        lax.fori_loop(0, NCH, body, 0)

    last = GROUPS - 1
    up_step(0, ())
    send_c(0)
    up_step(1, ((0, send_o, 0), (3, send_i, 0)))
    send_c(1)
    up_step(2, ((0, send_o, 1), (1, send_z, 0), (3, send_i, 1)))
    send_c(2)
    up_step(3, ((0, send_o, 2), (1, send_z, 1), (3, send_i, 2)))
    send_c(3)
    pl.when(sums)(functools.partial(send_o, last))

    stages = (
        (0, send_z, (2,)),
        (1, send_y, (0, 1)),
        (2, send_y, (2,)),
        (3, send_i, (3,)),
        (4, send_az, (0, 1, 2)),
        (5, send_z, (3,)),
        (7, send_y, (3,)),
        (7, send_ai, (0, 1, 2)),
        (9, send_az, (3,)),
        (9, send_ao, (0, 1, 2)),
        (11, send_ai, (3,)),
        (12, send_ac, (0, 1, 2)),
        (13, send_ao, (3,)),
        (14, finish, (0, 1, 2)),
        (15, send_ac, (3,)),
    )

    def genome_step(i, _):
        for way in range(2):
            genome_copy(i, way, 0).wait_recv()
        block = ds(i * gch, gch, gch)
        a_prev = gelu(g_prev[block].astype(F32) * has_prev).astype(BF16)
        a_next = gelu(g_next[block].astype(F32) * has_next).astype(BF16)
        conv = dot(a_prev, w[0]) + dot(act[block], w[1]) + dot(a_next, w[2])
        ob[block] = (g[block].astype(F32) + conv).astype(BF16)
        out_copy(i).start()
        staged(i, stages)
        pl.when(jnp.logical_and(moves, i == EARLY - 2))(functools.partial(go_on, EARLY, LATE, range(last)))
        pl.when(jnp.logical_and(moves, i == LATE - 2))(functools.partial(go_on, LATE, NGC, (last,)))
        return 0

    lax.fori_loop(0, NGC, genome_step, 0)
    finish(last)

    def drain_up(i, _):
        gg_copy(i).wait()

        @pl.when(moves)
        def _():
            for j in range(GROUPS):
                for way in range(2):
                    for c_ in range(2):
                        up_copy(j, i, way, c_).wait_send()

        @pl.when(sums)
        def _():
            for j in range(GROUPS):
                up_handed(j, i).wait_send()

        return 0

    lax.fori_loop(0, NCH, drain_up, 0)

    def drain_genome(i, _):
        out_copy(i).wait()

        @pl.when(moves)
        def _():
            for way in range(2):
                for c_ in range(2):
                    genome_copy(i, way, c_).wait_send()

        @pl.when(sums)
        def _():
            genome_handed(i).wait_send()

        return 0

    lax.fori_loop(0, NGC, drain_genome, 0)

    @pl.when(moves)
    def _():
        for j in range(GROUPS):
            for k in range(nx):
                c_copy(j, k).wait_send()

    @pl.when(sums)
    def _():
        for j in range(GROUPS):
            for k in range(2):
                o_copy(j, k).wait_send()
                ao_copy(j, k, d).wait_send()
            i_copy(j).wait_send()
            ai_copy(j, x).wait_send()
            for k, x_ in enumerate((2 * (1 - d), 2 * (1 - d) + 1, inner_x, x)):
                ac_copy(j, k, x_).wait_send()
            for k in range(nz - 1):
                z_copy(j, k).wait_send()
                az_copy(j, k, z).wait_send()
            for k in range(ny - 1):
                y_copy(j, k, y).wait_send()

    for j in range(GROUPS):
        gw_copy(j).wait()


def per_device(dims, genome, conv_weight, upstream):
    nz, nxl, ny, nd = dims
    nx = nxl * nd
    _, bins, chans = genome.shape
    rows, wide = 3 * chans, chans // GROUPS
    hop = DILATION_BINS // bins
    dma = pltpu.SemaphoreType.DMA
    block = pltpu.VMEM((bins, chans), BF16)
    out, grad_genome, grad_weight = pl.pallas_call(
        functools.partial(kernel, dims, hop),
        out_shape=(
            jax.ShapeDtypeStruct((bins, chans), BF16),
            jax.ShapeDtypeStruct((bins, chans), BF16),
            jax.ShapeDtypeStruct((rows, chans), BF16),
        ),
        in_specs=[pl.BlockSpec(memory_space=pltpu.HBM)] * 3,
        out_specs=(pl.BlockSpec(memory_space=pl.ANY),) * 3,
        scratch_shapes=[
            block, block,
            pltpu.VMEM((3, chans, chans), BF16),
            block, block, block, block, block, block, block,
            pltpu.VMEM((chans, bins), BF16),
            block, block,
            pltpu.VMEM((GROUPS, rows, wide), F32),
            pltpu.VMEM((GROUPS, rows, wide), F32),
            pltpu.VMEM((GROUPS, 2, rows // nx, wide), F32),
            pltpu.VMEM((GROUPS, 2, rows // nx, wide), F32),
            pltpu.VMEM((GROUPS, rows // nx, wide), BF16),
            pltpu.VMEM((GROUPS, rows // nx, wide), BF16),
            pltpu.VMEM((GROUPS, rows // nx, wide), F32),
            pltpu.VMEM((GROUPS, rows // nx, wide), BF16),
            pltpu.VMEM((GROUPS, nz - 1, rows // nx // nz, wide), BF16),
            pltpu.VMEM((GROUPS, ny, rows // nx // nz, wide), F32),
            pltpu.VMEM((rows, chans), BF16),
            dma((3,)),
            dma((GROUPS, NCH)), dma((GROUPS, NCH)),
            dma((NGC,)), dma((NGC,)),
            dma((2, 2, GROUPS, NCH)), dma((2, GROUPS, NCH)),
            dma((2, 2, NGC)), dma((2, NGC)),
            dma((NGC,)), dma((NCH,)), dma((GROUPS,)),
            dma((GROUPS, nx)), dma((GROUPS, nx)),
            dma((GROUPS, 2)), dma((GROUPS, 2)),
            dma((GROUPS,)), dma((GROUPS,)),
            dma((GROUPS, nz - 1)), dma((GROUPS, nz - 1)),
            dma((GROUPS, ny - 1)), dma((GROUPS, ny - 1)),
            dma((GROUPS, nz - 1)), dma((GROUPS, nz - 1)),
            dma((GROUPS,)), dma((GROUPS,)),
            dma((GROUPS, 2)), dma((GROUPS, 2)),
            dma((GROUPS, nx)), dma((GROUPS, nx)),
            pltpu.SemaphoreType.REGULAR((GROUPS,)),
        ],
        compiler_params=pltpu.CompilerParams(
            collective_id=0, has_side_effects=True, vmem_limit_bytes=VMEM_MIB * 1024 * 1024
        ),
    )(*(pltpu.with_memory_space_constraint(a, pltpu.HBM) for a in (genome[0], conv_weight, upstream[0])))
    return out[None], grad_genome[None], grad_weight.reshape(3, chans, chans).astype(F32)


def solution(mesh):
    ny, nxl, nc = 4, 2, 2
    nz = mesh.shape["seq"] // (ny * nxl * nc)
    return jax.shard_map(
        functools.partial(per_device, (nz, nxl, ny, mesh.shape["dp"])),
        mesh=mesh,
        in_specs=(P("dp", "seq", None), P(), P("dp", "seq", None)),
        out_specs=(P("dp", "seq", None), P("dp", "seq", None), P()),
        check_vma=False,
    )
```

```python
import functools

import jax
import jax.numpy as jnp
from jax import lax
from jax.experimental import pallas as pl
from jax.experimental.pallas import tpu as pltpu
from jax.sharding import PartitionSpec as P

MESH = pl.DeviceIdType.MESH
F32 = jnp.float32
BF16 = jnp.bfloat16
DILATION_BINS = 4096
NCH = 4
NGC = 16
GROUPS = 4
AHEAD = 4
VMEM_MIB = 46
CUBIC = 0.044715
SLOPE = 0.7978845608028654


def gelu(x):
    return x * (0.5 * (1.0 + jnp.tanh(SLOPE * (x + CUBIC * (x * x * x)))))


def gelu_slope(x):
    square = x * x
    t = jnp.tanh(SLOPE * (x + CUBIC * (x * square)))
    return 0.5 * (1.0 + t) + (0.5 * SLOPE) * x * (1.0 - t * t) * (1.0 + (3.0 * CUBIC) * square)


def dot(a, b):
    return jnp.dot(a, b, preferred_element_type=F32)


def dot_nt(a, b):
    return lax.dot_general(a, b, (((1,), (1,)), ((), ())), preferred_element_type=F32)


def kernel(
    dims, hop,
    g_hbm, w_hbm, u_hbm, out_hbm, gg_hbm, gw_hbm,
    g, u, w, u_other, g_other, u_prev, u_next, g_prev, g_next, act, act_t, ob, gb,
    acc, rc, os_, orx, is_, irx, zf, zs, rz, ry, yh, ag,
    lsem, ous, our, ogs, ogr, us, ur, gs, gr, osem, gsem, wsem,
    cs, cr, oss, osr, iss, isr, zss, zr, yss, yr, azs, azr, ais, air, aos, aor, acs, acr, yhs, yhr,
):
    nz, nxl, ny, nd = dims
    nx = nxl * nd
    ns = nz * nxl * ny * 2
    bins, chans = g.shape
    rows = 3 * chans
    rx_rows = rows // nx
    rz_rows = rx_rows // nz
    ch, gch = bins // NCH, bins // NGC
    wide = chans // GROUPS

    s = lax.axis_index("seq")
    d = lax.axis_index("dp")
    core = lax.rem(s, 2)
    y = lax.rem(lax.div(s, 2), ny)
    xl = lax.rem(lax.div(s, 2 * ny), nxl)
    z = lax.div(s, 2 * ny * nxl)
    x = d * nxl + xl
    base = s - core
    moves, sums = core == 0, core == 1

    def at(z_, x_, y_, c_):
        return {
            "dp": lax.div(x_, nxl),
            "seq": ((z_ * nxl + lax.rem(x_, nxl)) * ny + y_) * 2 + c_,
        }

    def beside(way, c_):
        return {"dp": d, "seq": lax.rem(base + (hop, ns - hop)[way], ns) + c_}

    partner = at(z, x, y, 1 - core)

    outer_x = lax.rem(x + 3 - 2 * xl, nx)
    inner_x = x + 1 - 2 * xl
    outer, inner = at(z, outer_x, y, core), at(z, inner_x, y, core)

    def z_at(k):
        return lax.rem(z + 1 + k, nz)

    def z_from(k):
        return lax.rem(z + 2 * nz - 1 - k, nz)

    def y_at(k):
        return lax.rem(y + 1 + k, ny)

    def y_from(k):
        return lax.rem(y + 2 * ny - 1 - k, ny)

    z_peers = [at(z_at(k), x, y, core) for k in range(nz - 1)]
    y_peers = [at(z, x, y_at(k), 1) for k in range(ny - 1)]
    y_movers = [at(z, x, y_at(k), 0) for k in range(ny - 1)]

    def ds(start, size, step):
        return pl.ds(pl.multiple_of(start, step), size)

    def remote(src, dst, send, recv, device):
        return pltpu.make_async_remote_copy(
            src_ref=src, dst_ref=dst, send_sem=send, recv_sem=recv, device_id=device, device_id_type=MESH
        )

    loads = [
        pltpu.make_async_copy(g_hbm, g, lsem.at[0]),
        pltpu.make_async_copy(u_hbm, u, lsem.at[1]),
        pltpu.make_async_copy(w_hbm, w, lsem.at[2]),
    ]
    for load in loads:
        load.start()

    barrier = pltpu.get_barrier_semaphore()

    def greet(devices):
        for device in devices:
            pl.semaphore_signal(barrier, inc=1, device_id=device, device_id_type=MESH)

    greet([partner, beside(0, 0), beside(1, 0)])
    sum_peers = z_peers + [outer, inner]

    @pl.when(moves)
    def _():
        pl.semaphore_wait(barrier, 5 + len(y_movers))

    @pl.when(sums)
    def _():
        greet(sum_peers + y_movers)
        pl.semaphore_wait(barrier, 1 + len(sum_peers))

    def columns(j):
        return pl.ds(j * wide, wide)

    def up_block(j, i):
        return (ds(i * ch, ch, ch), columns(j))

    def up_copy(j, i, way, c_):
        block = up_block(j, i)
        src, dst = (u_hbm, u_other)[c_], (u_prev, u_next)[way]
        return remote(
            src.at[block], dst.at[block], us.at[c_, way, j, i], ur.at[way, j, i], beside(way, c_)
        )

    def up_handed(j, i):
        block = up_block(j, i)
        return remote(u_hbm.at[block], u_other.at[block], ous.at[j, i], our.at[j, i], partner)

    def genome_copy(i, way, c_):
        block = ds(i * gch, gch, gch)
        src, dst = (g_hbm, g_other)[c_], (g_prev, g_next)[way]
        return remote(src.at[block], dst.at[block], gs.at[c_, way, i], gr.at[way, i], beside(way, c_))

    def genome_handed(i):
        block = ds(i * gch, gch, gch)
        return remote(g_hbm.at[block], g_other.at[block], ogs.at[i], ogr.at[i], partner)

    @pl.when(sums)
    def _():
        for j in range(GROUPS):

            def hand_up(i, _, j=j):
                up_handed(j, i).start()
                return 0

            lax.fori_loop(0, NCH, hand_up, 0)

        def hand_genome(i, _):
            genome_handed(i).start()
            return 0

        lax.fori_loop(0, NGC, hand_genome, 0)

    @pl.when(moves)
    def _():
        for j in range(GROUPS):

            def send_up(i, _, j=j):
                for way in range(2):
                    up_copy(j, i, way, 0).start()
                up_handed(j, i).wait_recv()
                for way in range(2):
                    up_copy(j, i, way, 1).start()
                return 0

            lax.fori_loop(0, NCH, send_up, 0)

    def x_block(x_):
        return ds(x_ * rx_rows, rx_rows, rx_rows)

    def z_block(z_):
        return ds(z_ * rz_rows, rz_rows, rz_rows)

    def c_block(k):
        return x_block((2 * (1 - d), 2 * (1 - d) + 1, inner_x, x)[k])

    def c_copy(j, k):
        block = c_block(k)
        return remote(acc.at[j, block], rc.at[j, block], cs.at[j, k], cr.at[j, k], partner)

    def o_copy(j, k):
        return remote(os_.at[j, k], orx.at[j, k], oss.at[j, k], osr.at[j, k], outer)

    def i_copy(j):
        return remote(is_.at[j], irx.at[j], iss.at[j], isr.at[j], inner)

    def z_copy(j, k):
        return remote(zs.at[j, z_block(z_at(k))], rz.at[j, k], zss.at[j, k], zr.at[j, k], z_peers[k])

    def y_copy(j, k, slot):
        return remote(yh.at[j], ry.at[j, slot], yss.at[j, k], yr.at[j, k], y_peers[k])

    def y_handed(j):
        return remote(ry.at[j, y], yh.at[j], yhs.at[j], yhr.at[j], partner)

    def az_copy(j, k, z_):
        block = ag.at[ds(x * rx_rows + z_ * rz_rows, rz_rows, rz_rows), columns(j)]
        return remote(block, block, azs.at[j, k], azr.at[j, k], z_peers[k])

    def ai_copy(j, x_):
        block = ag.at[x_block(x_), columns(j)]
        return remote(block, block, ais.at[j], air.at[j], inner)

    def ao_copy(j, k, d_):
        block = ag.at[x_block(2 * d_ + k), columns(j)]
        return remote(block, block, aos.at[j, k], aor.at[j, k], outer)

    def ac_copy(j, k, x_):
        block = ag.at[x_block(x_), columns(j)]
        return remote(block, block, acs.at[j, k], acr.at[j, k], partner)

    def send_c(j):
        @pl.when(moves)
        def _():
            for k in range(nx):
                c_copy(j, k).start()

    def send_o(j):
        for k in range(2):
            c_copy(j, k).wait_recv()
            block = c_block(k)
            os_[j, k] = acc[j, block] + rc[j, block]
            o_copy(j, k).start()

    def send_i(j):
        c_copy(j, 2).wait_recv()
        o_copy(j, 1 - xl).wait_recv()
        block = c_block(2)
        is_[j] = (acc[j, block] + rc[j, block] + orx[j, 1 - xl]).astype(BF16)
        i_copy(j).start()

    def send_z(j):
        c_copy(j, 3).wait_recv()
        o_copy(j, xl).wait_recv()
        i_copy(j).wait_recv()
        block = c_block(3)
        total = acc[j, block] + rc[j, block] + orx[j, xl] + irx[j].astype(F32)
        zf[j] = total
        zs[j] = total.astype(BF16)
        for k in range(nz - 1):
            z_copy(j, k).start()

    def send_y(j):
        for k in range(nz - 1):
            z_copy(j, k).wait_recv()
        total = zf[j, z_block(z)]
        for k in range(nz - 1):
            total += rz[j, k].astype(F32)
        ry[j, y] = total
        y_handed(j).start()

    def pass_y(j):
        y_handed(j).wait_recv()
        for k in range(ny - 1):
            y_copy(j, k, y).start()

    def send_az(j):
        for k in range(ny - 1):
            y_copy(j, k, y_from(k)).wait_recv()
        total = ry[j, 0]
        for k in range(1, ny):
            total += ry[j, k]
        ag[ds(x * rx_rows + z * rz_rows, rz_rows, rz_rows), columns(j)] = total.astype(BF16)
        for k in range(nz - 1):
            az_copy(j, k, z).start()

    def send_ai(j):
        for k in range(nz - 1):
            az_copy(j, k, z_from(k)).wait_recv()
        ai_copy(j, x).start()
        ao_copy(j, xl, d).start()
        ac_copy(j, 3, x).start()

    def send_ao(j):
        ai_copy(j, inner_x).wait_recv()
        ao_copy(j, 1 - xl, d).start()
        ac_copy(j, 2, inner_x).start()

    def send_ac(j):
        for k in range(2):
            ao_copy(j, k, 1 - d).wait_recv()
            ac_copy(j, k, 2 * (1 - d) + k).start()

    def gw_copy(j):
        return pltpu.make_async_copy(ag.at[:, columns(j)], gw_hbm.at[:, columns(j)], wsem.at[j])

    def finish(j):
        @pl.when(moves)
        def _():
            for k, x_ in enumerate((2 * (1 - d), 2 * (1 - d) + 1, inner_x, x)):
                ac_copy(j, k, x_).wait_recv()

        gw_copy(j).start()

    has_prev = jnp.where(s >= hop, 1.0, 0.0).astype(F32)
    has_next = jnp.where(s < ns - hop, 1.0, 0.0).astype(F32)

    for load in loads:
        load.wait()
    acc[...] = jnp.zeros_like(acc)

    def own(i, _):
        block = ds(i * gch, gch, gch)
        a = gelu(g[block].astype(F32))
        act[block] = a.astype(BF16)
        act_t[:, block] = a.T.astype(BF16)
        return 0

    lax.fori_loop(0, NGC, own, 0)

    def send_genome(i, _):
        for way in range(2):
            genome_copy(i, way, 0).start()
        genome_handed(i).wait_recv()
        for way in range(2):
            genome_copy(i, way, 1).start()
        return 0

    @pl.when(moves)
    def _():
        lax.fori_loop(0, AHEAD, send_genome, 0)

    def masked(ref, index, there):
        value = ref[index]
        return value * jnp.full(value.shape, there, F32).astype(BF16)

    def gg_copy(i):
        block = ds(i * ch, ch, ch)
        return pltpu.make_async_copy(gb.at[block], gg_hbm.at[block], gsem.at[i])

    def out_copy(i):
        block = ds(i * gch, gch, gch)
        return pltpu.make_async_copy(ob.at[block], out_hbm.at[block], osem.at[i])

    def staged(i, stages):
        for tick, stage, groups in stages:
            when = i == tick
            when = jnp.logical_and(when, moves if stage is pass_y else sums)

            @pl.when(when)
            def _(stage=stage, groups=groups):
                for j in groups if isinstance(groups, tuple) else (groups,):
                    stage(j)

    def up_step(j, stages):
        def body(i, _):
            for way in range(2):
                up_copy(j, i, way, 0).wait_recv()
            block, side = up_block(j, i)
            left = act_t[:, block]
            for tap, right in (
                (0, masked(u_next, (block, side), has_next)),
                (1, u[block, side]),
                (2, masked(u_prev, (block, side), has_prev)),
            ):
                acc[j, pl.ds(tap * chans, chans)] += dot(left, right)
            if j == GROUPS - 1:
                own_up = u[block]
                grad_act = (
                    dot_nt(masked(u_next, block, has_next), w[0])
                    + dot_nt(own_up, w[1])
                    + dot_nt(masked(u_prev, block, has_prev), w[2])
                )
                slope = gelu_slope(g[block].astype(F32))
                gb[block] = (own_up.astype(F32) + slope * grad_act).astype(BF16)
                gg_copy(i).start()
            staged(i, stages)
            return 0

        lax.fori_loop(0, NCH, body, 0)

    last = GROUPS - 1
    up_step(0, ())
    send_c(0)
    up_step(1, ((0, send_o, 0), (3, send_i, 0)))
    send_c(1)
    up_step(2, ((0, send_o, 1), (1, send_z, 0), (3, send_i, 1)))
    send_c(2)
    up_step(3, ((0, send_o, 2), (1, send_z, 1), (3, send_i, 2)))
    send_c(3)
    pl.when(sums)(functools.partial(send_o, last))

    stages = (
        (0, send_z, (2,)),
        (2, send_y, (0, 1, 2)),
        (3, pass_y, (0, 1, 2)),
        (3, send_i, (3,)),
        (5, send_z, (3,)),
        (7, send_y, (3,)),
        (7, pass_y, (3,)),
        (9, send_az, (0, 1, 2)),
        (11, send_ai, (0, 1, 2)),
        (13, send_ao, (0, 1, 2)),
        (13, send_az, (3,)),
        (15, send_ac, (0, 1, 2)),
        (15, send_ai, (3,)),
    )

    def genome_step(i, _):
        for way in range(2):
            genome_copy(i, way, 0).wait_recv()

        @pl.when(jnp.logical_and(moves, i + AHEAD < NGC))
        def _():
            send_genome(i + AHEAD, 0)

        block = ds(i * gch, gch, gch)
        a_prev = gelu(g_prev[block].astype(F32) * has_prev).astype(BF16)
        a_next = gelu(g_next[block].astype(F32) * has_next).astype(BF16)
        conv = dot(a_prev, w[0]) + dot(act[block], w[1]) + dot(a_next, w[2])
        ob[block] = (g[block].astype(F32) + conv).astype(BF16)
        out_copy(i).start()
        staged(i, stages)
        return 0

    lax.fori_loop(0, NGC, genome_step, 0)

    @pl.when(sums)
    def _():
        send_ao(last)
        send_ac(last)

    for j in range(GROUPS):
        finish(j)

    def drain_up(i, _):
        gg_copy(i).wait()

        @pl.when(moves)
        def _():
            for j in range(GROUPS):
                for way in range(2):
                    for c_ in range(2):
                        up_copy(j, i, way, c_).wait_send()

        @pl.when(sums)
        def _():
            for j in range(GROUPS):
                up_handed(j, i).wait_send()

        return 0

    lax.fori_loop(0, NCH, drain_up, 0)

    def drain_genome(i, _):
        out_copy(i).wait()

        @pl.when(moves)
        def _():
            for way in range(2):
                for c_ in range(2):
                    genome_copy(i, way, c_).wait_send()

        @pl.when(sums)
        def _():
            genome_handed(i).wait_send()

        return 0

    lax.fori_loop(0, NGC, drain_genome, 0)

    @pl.when(moves)
    def _():
        for j in range(GROUPS):
            for k in range(nx):
                c_copy(j, k).wait_send()
            for k in range(ny - 1):
                y_copy(j, k, y).wait_send()

    @pl.when(sums)
    def _():
        for j in range(GROUPS):
            for k in range(2):
                o_copy(j, k).wait_send()
                ao_copy(j, k, d).wait_send()
            i_copy(j).wait_send()
            ai_copy(j, x).wait_send()
            for k, x_ in enumerate((2 * (1 - d), 2 * (1 - d) + 1, inner_x, x)):
                ac_copy(j, k, x_).wait_send()
            for k in range(nz - 1):
                z_copy(j, k).wait_send()
                az_copy(j, k, z).wait_send()
            y_handed(j).wait_send()

    for j in range(GROUPS):
        gw_copy(j).wait()


def per_device(dims, genome, conv_weight, upstream):
    nz, nxl, ny, nd = dims
    nx = nxl * nd
    _, bins, chans = genome.shape
    rows, wide = 3 * chans, chans // GROUPS
    hop = DILATION_BINS // bins
    dma = pltpu.SemaphoreType.DMA
    block = pltpu.VMEM((bins, chans), BF16)
    out, grad_genome, grad_weight = pl.pallas_call(
        functools.partial(kernel, dims, hop),
        out_shape=(
            jax.ShapeDtypeStruct((bins, chans), BF16),
            jax.ShapeDtypeStruct((bins, chans), BF16),
            jax.ShapeDtypeStruct((rows, chans), BF16),
        ),
        in_specs=[pl.BlockSpec(memory_space=pltpu.HBM)] * 3,
        out_specs=(pl.BlockSpec(memory_space=pl.ANY),) * 3,
        scratch_shapes=[
            block, block,
            pltpu.VMEM((3, chans, chans), BF16),
            block, block, block, block, block, block, block,
            pltpu.VMEM((chans, bins), BF16),
            block, block,
            pltpu.VMEM((GROUPS, rows, wide), F32),
            pltpu.VMEM((GROUPS, rows, wide), F32),
            pltpu.VMEM((GROUPS, 2, rows // nx, wide), F32),
            pltpu.VMEM((GROUPS, 2, rows // nx, wide), F32),
            pltpu.VMEM((GROUPS, rows // nx, wide), BF16),
            pltpu.VMEM((GROUPS, rows // nx, wide), BF16),
            pltpu.VMEM((GROUPS, rows // nx, wide), F32),
            pltpu.VMEM((GROUPS, rows // nx, wide), BF16),
            pltpu.VMEM((GROUPS, nz - 1, rows // nx // nz, wide), BF16),
            pltpu.VMEM((GROUPS, ny, rows // nx // nz, wide), F32),
            pltpu.VMEM((GROUPS, rows // nx // nz, wide), F32),
            pltpu.VMEM((rows, chans), BF16),
            dma((3,)),
            dma((GROUPS, NCH)), dma((GROUPS, NCH)),
            dma((NGC,)), dma((NGC,)),
            dma((2, 2, GROUPS, NCH)), dma((2, GROUPS, NCH)),
            dma((2, 2, NGC)), dma((2, NGC)),
            dma((NGC,)), dma((NCH,)), dma((GROUPS,)),
            dma((GROUPS, nx)), dma((GROUPS, nx)),
            dma((GROUPS, 2)), dma((GROUPS, 2)),
            dma((GROUPS,)), dma((GROUPS,)),
            dma((GROUPS, nz - 1)), dma((GROUPS, nz - 1)),
            dma((GROUPS, ny - 1)), dma((GROUPS, ny - 1)),
            dma((GROUPS, nz - 1)), dma((GROUPS, nz - 1)),
            dma((GROUPS,)), dma((GROUPS,)),
            dma((GROUPS, 2)), dma((GROUPS, 2)),
            dma((GROUPS, nx)), dma((GROUPS, nx)),
            dma((GROUPS,)), dma((GROUPS,)),
        ],
        compiler_params=pltpu.CompilerParams(
            collective_id=0, has_side_effects=True, vmem_limit_bytes=VMEM_MIB * 1024 * 1024
        ),
    )(*(pltpu.with_memory_space_constraint(a, pltpu.HBM) for a in (genome[0], conv_weight, upstream[0])))
    return out[None], grad_genome[None], grad_weight.reshape(3, chans, chans).astype(F32)


def solution(mesh):
    ny, nxl, nc = 4, 2, 2
    nz = mesh.shape["seq"] // (ny * nxl * nc)
    return jax.shard_map(
        functools.partial(per_device, (nz, nxl, ny, mesh.shape["dp"])),
        mesh=mesh,
        in_specs=(P("dp", "seq", None), P(), P("dp", "seq", None)),
        out_specs=(P("dp", "seq", None), P("dp", "seq", None), P()),
        check_vma=False,
    )
```
